128 devices in a mesh: row: 8 (over y, core), col: 16 (over z, x).
Axes of the slice: x: 4, y: 4, z: 4, core: 2. Of those that a mesh axis runs over, the one named last changes fastest.
Arguments:
- kernel_panel: float32 [64, 32768], P(None, ('row', 'col')), may hold values from -4 to 16, as said below
- kernel_slab: float32 [32768, 4096], P('row', 'col'), may hold values from -4 to 20, as said below
- targets: float32 [256, 32768], P(None, ('row', 'col')), may hold values from -6 to 6
Outputs:
- updated_slab: float32 [32768, 4096], P('row', 'col')
- solved_targets: float32 [256, 32768], P('col', 'row')
- panel_factor: float32 [64, 32768], P(None, ('row', 'col'))
The draws below stay inside these ranges and needn't reach their ends.
Inputs may be any that keep to these rules, and one draw needn't show every extreme that they name: kernel_panel[:, 0:64] is symmetric and positive definite. `kernel_slab`: rows 0 to 63 equal kernel_panel[:, 32768 - 4096 : 32768]; the last 4096 rows form a symmetric matrix.
All inputs are finite; a program needn't handle non-finite values.
Results may differ from the reference program's by a relative error of at most 0.00018.
Values sent between devices are 32-bit elements; how exact they have to be, the bound alone decides.
No kernel may reach another device: no remote copies, remote signals or barrier semaphores. Data moves between devices by JAX's collectives and lax.ppermute only.
A program may use at most 64 MiB of HBM per device.

```python
import math
import jax
import jax.numpy as jnp
from jax import lax

PANEL = 64
SLAB = 4096
TGT = 256
NR = 32768


def panel_core(key):
    keys = jax.random.split(jax.random.fold_in(key, 7), 5)
    jitter = jax.random.uniform(keys[0], (PANEL,), jnp.float32, -0.4, 0.4)
    points = jnp.arange(PANEL, dtype=jnp.float32) + jitter
    length_scale = 3.0
    amplitude = jnp.exp(jax.random.uniform(keys[1], (PANEL,), jnp.float32, 0.0, math.log(2.0)))
    nugget = jnp.exp(jax.random.uniform(keys[4], (PANEL,), jnp.float32, 0.0, math.log(4.0)))
    spacing = (points[:, None] - points[None, :]) / length_scale
    gram = amplitude[:, None] * amplitude[None, :] * jnp.exp(-0.5 * spacing * spacing)
    identity = jnp.eye(PANEL, dtype=jnp.float32)
    corner = gram + identity * nugget[None, :]
    remain = 0.5 * jax.random.truncated_normal(keys[2], -4.0, 4.0, (PANEL, NR - PANEL), jnp.float32)
    return jnp.concatenate([corner, remain], 1)


def draw_kernel_panel(key, part):
    return panel_core(key)


def draw_kernel_slab(key, part):
    keys = jax.random.split(jax.random.fold_in(key, 13), 2)
    base = jax.random.truncated_normal(keys[0], -4.0, 4.0, (NR, SLAB), jnp.float32)
    square = base[NR - SLAB:]
    diag_values = jnp.exp(jax.random.uniform(keys[1], (SLAB,), jnp.float32, math.log(8.0), math.log(16.0)))
    square = 0.5 * (square + square.T) + jnp.eye(SLAB, dtype=jnp.float32) * diag_values[None, :]
    head_rows = panel_core(key)[:, NR - SLAB:]
    return jnp.concatenate([head_rows, base[PANEL:NR - SLAB], square], 0)


def steps_of(key, shape, shards, smallest, high):
    def one(position, shards_of):
        draws = jax.random.uniform(jax.random.fold_in(jax.random.fold_in(key, 6), position), (shards_of,), jnp.float32, smallest / len(shards), high / len(shards))
        return jnp.repeat(jnp.exp(draws), shape[position] // shards_of).reshape((-1,) + (1,) * (len(shape) - position - 1))

    factor_of = one(*shards[0])
    for cut in shards[1:]:
        factor_of = factor_of * one(*cut)
    return factor_of


def centred(stream_key, shape, spread, most, cuts=(), kind=jnp.bfloat16):
    values = jax.random.normal(stream_key, shape, jnp.float32) * spread
    if len(cuts) > 0:
        values = steps_of(stream_key, shape, cuts, -0.22, 0.18) * values
    return jnp.clip(values, min=-most, max=most).astype(kind)


def setup_inputs(seed: int = 0) -> dict:
    seeds = jax.random.split(jax.random.key(seed), 4)
    return {
        "kernel_panel": draw_kernel_panel(jax.random.fold_in(seeds[3], 71), 0),
        "kernel_slab": draw_kernel_slab(jax.random.fold_in(seeds[3], 71), 0),
        "targets": centred(seeds[2], (TGT, NR), 1.0, 6.0, ((1, 128),), jnp.float32),
    }


def lower_solve(factor, values):
    return jax.scipy.linalg.solve_triangular(factor, values, lower=True)

def reference(kernel_panel, kernel_slab, targets):
    lower_factor = jnp.linalg.cholesky(kernel_panel[:, :PANEL])
    panel_factor = lower_solve(lower_factor, kernel_panel)
    slab_factor = panel_factor[:, NR - SLAB:]
    product = lax.dot_general(panel_factor.astype(jnp.float32), slab_factor.astype(jnp.float32), (((0,), (0,)), ((), ())), precision=lax.Precision.HIGHEST, preferred_element_type=jnp.float32)
    update = kernel_slab - product
    updated_slab = jnp.concatenate([slab_factor, update[PANEL:]], 0)
    solved_lead = lower_solve(lower_factor, targets[:, :PANEL].T).T
    result = targets - jnp.dot(solved_lead.astype(jnp.float32), panel_factor.astype(jnp.float32), precision=lax.Precision.HIGHEST, preferred_element_type=jnp.float32)
    solved_targets = jnp.concatenate([solved_lead, result[:, PANEL:]], 1)
    return (updated_slab, solved_targets, panel_factor)
```

```python
import jax
import jax.numpy as jnp
from jax import lax
from jax.sharding import PartitionSpec as P

HIGHEST = lax.Precision.HIGHEST


def lower_solve(factor, values):
    return jax.scipy.linalg.solve_triangular(factor, values, lower=True)


def from_first(value, axis):
    size, index = lax.axis_size(axis), lax.axis_index(axis)
    reach = size
    while reach > 1:
        half = reach // 2
        pairs = [(i, i + half) for i in range(0, size, reach)]
        arrived = lax.ppermute(value, axis, pairs)
        value = jnp.where(index % reach == half, arrived, value)
        reach = half
    return value


def body(kernel_panel, kernel_slab, targets):
    width = kernel_panel.shape[0]
    cols = lax.axis_size("col")
    row_index = lax.axis_index("row")
    col_index = lax.axis_index("col")
    wide = kernel_panel.shape[1]
    mine = targets.shape[0] // cols
    pieces = jnp.broadcast_to(kernel_panel[None], (cols,) + kernel_panel.shape)
    sent = jnp.concatenate([pieces, targets.reshape(cols, mine, wide)], 1)
    got = lax.all_to_all(sent, "col", split_axis=0, concat_axis=0)
    lead = jnp.concatenate([kernel_panel[:, :width], targets[:, :width].T], 1)
    down = from_first(jnp.concatenate([kernel_slab[:width], lead], 1), "row")
    slab_panel, lead = down[:, :wide], down[:, wide:]
    corner = jnp.broadcast_to(lead[:, :width][None], (cols, width, width))
    heads = lead[:, width:].reshape(width, cols, mine).transpose(1, 0, 2)
    small = lax.all_to_all(jnp.concatenate([corner, heads], 2), "col", split_axis=0, concat_axis=0)[0]
    lower_factor = jnp.linalg.cholesky(small[:, :width])
    raw = got[:, :width].transpose(1, 0, 2).reshape(width, cols * wide)
    solved = lower_solve(lower_factor, jnp.concatenate([raw, slab_panel, kernel_panel, small[:, width:]], 1))
    gathered = solved[:, : cols * wide]
    slab_factor = solved[:, cols * wide : cols * wide + wide]
    panel_factor = solved[:, cols * wide + wide : cols * wide + 2 * wide]
    solved_lead = solved[:, cols * wide + 2 * wide :].T
    product = lax.dot_general(
        gathered, slab_factor, (((0,), (0,)), ((), ())), precision=HIGHEST, preferred_element_type=jnp.float32
    )
    update = kernel_slab - product
    head_rows = jnp.where(row_index == 0, slab_factor, update[:width])
    updated_slab = jnp.concatenate([head_rows, update[width:]], 0)
    rows = got[:, width:].transpose(1, 0, 2).reshape(mine, cols * wide)
    result = rows - jnp.dot(solved_lead, gathered, precision=HIGHEST, preferred_element_type=jnp.float32)
    head_cols = jnp.where(row_index == 0, solved_lead, result[:, :width])
    solved_targets = jnp.concatenate([head_cols, result[:, width:]], 1)
    return (updated_slab, solved_targets, panel_factor)


def solution(mesh):
    in_specs = (P(None, ("row", "col")), P("row", "col"), P(None, ("row", "col")))
    out_specs = (P("row", "col"), P("col", "row"), P(None, ("row", "col")))
    return jax.shard_map(body, mesh=mesh, in_specs=in_specs, out_specs=out_specs, check_vma=False)
```

```python
import jax
import jax.numpy as jnp
from jax import lax
from jax.experimental import pallas as pl
from jax.experimental.pallas import tpu as pltpu
from jax.sharding import PartitionSpec as P

HIGHEST = lax.Precision.HIGHEST
LANES = 128
SUB = 8


def invert_kernel(lead_ref, inverse_ref):
    width = inverse_ref.shape[0]
    count = width // SUB
    lane = lax.broadcasted_iota(jnp.int32, (SUB, LANES), 1)
    row = lax.broadcasted_iota(jnp.int32, (SUB, LANES), 0)
    blocks = []
    for i in range(count):
        unit = jnp.where(lane - width == row + i * SUB, 1.0, 0.0).astype(jnp.float32)
        blocks.append(jnp.where(lane < width, lead_ref[i * SUB : (i + 1) * SUB, :], unit))
    shape = (SUB, LANES)
    for b in range(count):
        below = range(b + 1, count)
        spread = [
            {i: jnp.broadcast_to(blocks[i][:, b * SUB + j : b * SUB + j + 1], shape) for i in range(b, count)}
            for j in range(SUB)
        ]
        for j in range(SUB):
            pivot = jnp.broadcast_to(spread[j][b][j : j + 1, :], shape)
            scale = lax.rsqrt(pivot)
            scale = scale * (1.5 - 0.5 * (pivot * scale) * scale)
            top = jnp.broadcast_to(blocks[b][j : j + 1, :], shape) * scale
            factor = {i: spread[j][i] * scale for i in below}
            factor[b] = jnp.where(row > j, spread[j][b] * scale, 0.0)
            for k in range(j + 1, SUB):
                entry = jnp.broadcast_to(spread[k][b][j : j + 1, :], shape) * scale
                for i in range(b, count):
                    spread[k][i] = spread[k][i] - factor[i] * entry
            blocks[b] = jnp.where(row == j, top, blocks[b] - factor[b] * top)
            for i in below:
                blocks[i] = blocks[i] - factor[i] * top
    for i in range(count):
        inverse_ref[i * SUB : (i + 1) * SUB, :] = blocks[i][:, width:]


def invert(lead, width):
    return pl.pallas_call(
        invert_kernel,
        out_shape=jax.ShapeDtypeStruct((width, width), jnp.float32),
        in_specs=[pl.BlockSpec(memory_space=pltpu.VMEM)],
        out_specs=pl.BlockSpec(memory_space=pltpu.VMEM),
        cost_estimate=pl.CostEstimate(flops=4 * width**3, bytes_accessed=8 * width**2, transcendentals=width),
        name="invert_factor",
    )(lead)


def halves(value):
    high = value.astype(jnp.bfloat16)
    return high, (value - high.astype(jnp.float32)).astype(jnp.bfloat16)


def update_kernel(first_ref, one_ref, two_ref, inverse_ref, down_ref, panel_ref, slab_ref,
                  slab_out, targets_out, factor_out, held, arrive, leave):
    count, depth = one_ref.shape[0], one_ref.shape[1]
    width = inverse_ref.shape[0]
    wide = panel_ref.shape[1]
    pieces = [pl.ds(p * wide, wide) for p in range(count)]
    loads = [pltpu.make_async_copy(slab_ref.at[piece], held.at[piece], arrive.at[p]) for p, piece in enumerate(pieces)]
    stores = [pltpu.make_async_copy(held.at[piece], slab_out.at[piece], leave.at[p]) for p, piece in enumerate(pieces)]
    for load in loads:
        load.start()
    inverse = inverse_ref[...]

    def solve(values):
        return jnp.dot(inverse, values, precision=HIGHEST, preferred_element_type=jnp.float32)

    factor_out[...] = solve(panel_ref[...])
    slab_panel = jnp.concatenate([down_ref[depth : depth + width, :], down_ref[depth + width :, :]], 1)
    slab_factor = solve(slab_panel)
    slab_high, slab_low = halves(slab_factor)
    slab_stack = jnp.concatenate([slab_high, slab_low, slab_high], 0)
    lead = lax.dot_general(
        down_ref[width:depth, :width], inverse, (((1,), (1,)), ((), ())),
        precision=HIGHEST, preferred_element_type=jnp.float32,
    )
    is_first = first_ref[0] == 1
    for p in range(count):
        raw = jnp.concatenate([one_ref[p, :width, :], two_ref[p, :width, :]], 1)
        solved = solve(raw)
        high, low = halves(solved)
        stack = jnp.concatenate([high, high, low], 0)
        product = lax.dot_general(stack, slab_stack, (((0,), (0,)), ((), ())), preferred_element_type=jnp.float32)
        rest = jnp.concatenate([one_ref[p, width:, :], two_ref[p, width:, :]], 1)
        targets_out[:, p * wide : (p + 1) * wide] = rest - jnp.dot(
            lead, solved, precision=HIGHEST, preferred_element_type=jnp.float32
        )
        loads[p].wait()
        held[p * wide : (p + 1) * wide, :] = held[p * wide : (p + 1) * wide, :] - product
        if p == 0:

            @pl.when(is_first)
            def _():
                held[:width, :] = slab_factor
                targets_out[:, :width] = lead

        stores[p].start()
    for store in stores:
        store.wait()


def update(first, one, two, inverse, down, panel, slab):
    count, depth, _ = one.shape
    width, wide = panel.shape
    vmem = pl.BlockSpec(memory_space=pltpu.VMEM)
    hbm = pl.BlockSpec(memory_space=pl.ANY)
    return pl.pallas_call(
        update_kernel,
        out_shape=(
            jax.ShapeDtypeStruct(slab.shape, jnp.float32),
            jax.ShapeDtypeStruct((depth - width, count * wide), jnp.float32),
            jax.ShapeDtypeStruct(panel.shape, jnp.float32),
        ),
        in_specs=[pl.BlockSpec(memory_space=pltpu.SMEM), vmem, vmem, vmem, vmem, vmem, hbm],
        out_specs=(hbm, vmem, vmem),
        scratch_shapes=[
            pltpu.VMEM(slab.shape, jnp.float32),
            pltpu.SemaphoreType.DMA((count,)),
            pltpu.SemaphoreType.DMA((count,)),
        ],
        compiler_params=pltpu.CompilerParams(vmem_limit_bytes=24 << 20),
        cost_estimate=pl.CostEstimate(
            flops=6 * slab.size * width, bytes_accessed=8 * slab.size, transcendentals=0
        ),
        name="update_slab",
    )(first, one, two, inverse, down, panel, slab)


def from_first(value, axis):
    size, index = lax.axis_size(axis), lax.axis_index(axis)
    reach = size
    while reach > 1:
        half = reach // 2
        pairs = [(i, i + half) for i in range(0, size, reach)]
        arrived = lax.ppermute(value, axis, pairs)
        value = jnp.where(index % reach == half, arrived, value)
        reach = half
    return value


def body(kernel_panel, kernel_slab, targets):
    width, wide = kernel_panel.shape
    cols = lax.axis_size("col")
    mine = targets.shape[0] // cols

    def exchange(lo, hi):
        pieces = jnp.broadcast_to(kernel_panel[None, :, lo:hi], (cols, width, hi - lo))
        sent = jnp.concatenate([pieces, targets[:, lo:hi].reshape(cols, mine, hi - lo)], 1)
        return sent

    sent_one, sent_two = exchange(0, LANES), exchange(LANES, wide)
    one = lax.all_to_all(sent_one, "col", split_axis=0, concat_axis=0)
    two = lax.all_to_all(sent_two, "col", split_axis=0, concat_axis=0)
    down = jnp.concatenate([one[0], kernel_slab[:width, :LANES], kernel_slab[:width, LANES:]], 0)
    down = from_first(down, "row")
    inverse = invert(down[:width], width)
    first = (lax.axis_index("row") == 0).astype(jnp.int32).reshape(1)
    return tuple(update(first, one, two, inverse, down, kernel_panel, kernel_slab))


def solution(mesh):
    in_specs = (P(None, ("row", "col")), P("row", "col"), P(None, ("row", "col")))
    out_specs = (P("row", "col"), P("col", "row"), P(None, ("row", "col")))
    return jax.shard_map(body, mesh=mesh, in_specs=in_specs, out_specs=out_specs, check_vma=False)
```

```python
import jax
import jax.numpy as jnp
from jax import lax
from jax.experimental import pallas as pl
from jax.experimental.pallas import tpu as pltpu
from jax.sharding import PartitionSpec as P

HIGHEST = lax.Precision.HIGHEST
LANES = 128
SUB = 8
GROUPS = 4


def dot(left, right, dims=((1,), (0,))):
    return lax.dot_general(left, right, (dims, ((), ())), preferred_element_type=jnp.float32)


def exact(left, right, dims=((1,), (0,))):
    return lax.dot_general(left, right, (dims, ((), ())), precision=HIGHEST, preferred_element_type=jnp.float32)


def halves(value):
    high = value.astype(jnp.bfloat16)
    return high, (value - high.astype(jnp.float32)).astype(jnp.bfloat16)


def thirds(value):
    high = value.astype(jnp.bfloat16)
    rest = value - high.astype(jnp.float32)
    return (high, *halves(rest))


def inverse_factor(corner, width):
    count = width // SUB
    shape = (SUB, LANES)
    lane = lax.broadcasted_iota(jnp.int32, shape, 1)
    row = lax.broadcasted_iota(jnp.int32, shape, 0)
    blocks = []
    for i in range(count):
        part = corner[i * SUB : (i + 1) * SUB]
        unit = jnp.where(lane - width == row + i * SUB, 1.0, 0.0).astype(jnp.float32)
        blocks.append(jnp.where(lane < width, part, unit))
    for b in range(count):
        below = range(b + 1, count)
        spread = [
            {i: jnp.broadcast_to(blocks[i][:, b * SUB + j : b * SUB + j + 1], shape) for i in range(b, count)}
            for j in range(SUB)
        ]
        for j in range(SUB):
            pivot = jnp.broadcast_to(spread[j][b][j : j + 1, :], shape)
            scale = lax.rsqrt(pivot)
            scale = scale * (1.5 - 0.5 * (pivot * scale) * scale)
            top = jnp.broadcast_to(blocks[b][j : j + 1, :], shape) * scale
            factor = {i: spread[j][i] * scale for i in below}
            factor[b] = jnp.where(row > j, spread[j][b] * scale, 0.0)
            for k in range(j + 1, SUB):
                entry = jnp.broadcast_to(spread[k][b][j : j + 1, :], shape) * scale
                for i in range(b, count):
                    spread[k][i] = spread[k][i] - factor[i] * entry
            blocks[b] = jnp.where(row == j, top, blocks[b] - factor[b] * top)
            for i in below:
                blocks[i] = blocks[i] - factor[i] * top
    return jnp.concatenate([block[:, width:] for block in blocks], 0)


def step_kernel(first_ref, got_ref, lead_ref, slab_panel_ref, panel_ref, slab_ref,
                slab_out, targets_out, factor_out, held, pieces, stacks, arrive, leave, brought):
    count, _, wide = pieces.shape
    width = panel_ref.shape[0]
    each = count // GROUPS
    loads, stores = [], []
    for g in range(GROUPS):
        rows = pl.ds(g * each * wide, each * wide)
        loads.append(pltpu.make_async_copy(slab_ref.at[rows], held.at[rows], arrive.at[g]))
        stores.append(pltpu.make_async_copy(held.at[rows], slab_out.at[rows], leave.at[g]))
    bring = pltpu.make_async_copy(got_ref, pieces, brought)
    bring.start()
    for load in loads:
        load.start()
    is_first = first_ref[0] == 1
    inverse = inverse_factor(lead_ref[:width, :], width)
    slab_factor = exact(inverse, slab_panel_ref[...])
    high, low = halves(slab_factor)
    slab_stack = jnp.concatenate([high, low, high], 0)
    high, middle, low = thirds(inverse)
    large = jnp.concatenate([high, high, middle, middle], 1)
    small = jnp.concatenate([high, low], 1)
    bring.wait()
    for p in range(count):
        one, two, three = thirds(pieces[p, :width, :])
        solved = dot(large, jnp.concatenate([one, two, one, two], 0))
        solved = solved + dot(small, jnp.concatenate([three, one], 0))
        high, low = halves(solved)
        stacks[:, p * wide : (p + 1) * wide] = jnp.concatenate([high, high, low], 0)
    for g in range(GROUPS):
        loads[g].wait()
        for p in range(g * each, (g + 1) * each):
            product = dot(stacks[:, p * wide : (p + 1) * wide], slab_stack, ((0,), (0,)))
            held[p * wide : (p + 1) * wide, :] = held[p * wide : (p + 1) * wide, :] - product
        if g == 0:

            @pl.when(is_first)
            def _():
                held[:width, :] = slab_factor

        stores[g].start()
    lead = exact(lead_ref[width:, :width], inverse, ((1,), (1,)))
    high, low = halves(lead)
    lead_stack = jnp.concatenate([high, low, high], 1)
    factor_out[...] = exact(inverse, panel_ref[...])
    for p in range(count):
        product = dot(lead_stack, stacks[:, p * wide : (p + 1) * wide])
        targets_out[:, p * wide : (p + 1) * wide] = pieces[p, width:, :] - product

    @pl.when(is_first)
    def _():
        targets_out[:, :width] = lead

    for store in stores:
        store.wait()


def step(first, got, lead, slab_panel, panel, slab):
    count, depth, wide = got.shape
    width = panel.shape[0]
    vmem = pl.BlockSpec(memory_space=pltpu.VMEM)
    hbm = pl.BlockSpec(memory_space=pl.ANY)
    return pl.pallas_call(
        step_kernel,
        out_shape=(
            jax.ShapeDtypeStruct(slab.shape, jnp.float32),
            jax.ShapeDtypeStruct((depth - width, count * wide), jnp.float32),
            jax.ShapeDtypeStruct(panel.shape, jnp.float32),
        ),
        in_specs=[pl.BlockSpec(memory_space=pltpu.SMEM), hbm, vmem, vmem, vmem, hbm],
        out_specs=(hbm, vmem, vmem),
        scratch_shapes=[
            pltpu.VMEM(slab.shape, jnp.float32),
            pltpu.VMEM(got.shape, jnp.float32),
            pltpu.VMEM((3 * width, count * wide), jnp.bfloat16),
            pltpu.SemaphoreType.DMA((GROUPS,)),
            pltpu.SemaphoreType.DMA((GROUPS,)),
            pltpu.SemaphoreType.DMA(()),
        ],
        compiler_params=pltpu.CompilerParams(vmem_limit_bytes=56 << 20),
        cost_estimate=pl.CostEstimate(
            flops=6 * slab.size * width, bytes_accessed=8 * slab.size, transcendentals=width
        ),
        name="factor_and_update",
    )(first, got, lead, slab_panel, panel, slab)


def from_first(value, axis):
    size, index = lax.axis_size(axis), lax.axis_index(axis)
    reach = size
    while reach > 1:
        half = reach // 2
        pairs = [(i, i + half) for i in range(0, size, reach)]
        arrived = lax.ppermute(value, axis, pairs)
        value = jnp.where(index % reach == half, arrived, value)
        reach = half
    return value


def body(kernel_panel, kernel_slab, targets):
    width, wide = kernel_panel.shape
    cols = lax.axis_size("col")
    mine = targets.shape[0] // cols
    pieces = jnp.broadcast_to(kernel_panel[None], (cols, width, wide))
    sent = jnp.concatenate([pieces, targets.reshape(cols, mine, wide)], 1)
    got = lax.all_to_all(sent, "col", split_axis=0, concat_axis=0)
    slab_panel = from_first(kernel_slab[:width], "row")
    lead, slab_panel = lax.optimization_barrier((got[0, :, :LANES], slab_panel))
    lead = from_first(lead, "row")
    first = (lax.axis_index("row") == 0).astype(jnp.int32).reshape(1)
    return tuple(step(first, got, lead, slab_panel, kernel_panel, kernel_slab))


def solution(mesh):
    in_specs = (P(None, ("row", "col")), P("row", "col"), P(None, ("row", "col")))
    out_specs = (P("row", "col"), P("col", "row"), P(None, ("row", "col")))
    return jax.shard_map(body, mesh=mesh, in_specs=in_specs, out_specs=out_specs, check_vma=False)
```

```python
import jax
import jax.numpy as jnp
from jax import lax
from jax.experimental import pallas as pl
from jax.experimental.pallas import tpu as pltpu
from jax.sharding import PartitionSpec as P

HIGHEST = lax.Precision.HIGHEST
LANES = 128
SUB = 8
GROUPS = 4


def dot(left, right, dims=((1,), (0,))):
    return lax.dot_general(left, right, (dims, ((), ())), preferred_element_type=jnp.float32)


def exact(left, right, dims=((1,), (0,))):
    return lax.dot_general(left, right, (dims, ((), ())), precision=HIGHEST, preferred_element_type=jnp.float32)


def halves(value):
    high = value.astype(jnp.bfloat16)
    return high, (value - high.astype(jnp.float32)).astype(jnp.bfloat16)


def thirds(value):
    high = value.astype(jnp.bfloat16)
    rest = value - high.astype(jnp.float32)
    return (high, *halves(rest))


def inverse_factor(corner, width):
    count = width // SUB
    shape = (SUB, LANES)
    lane = lax.broadcasted_iota(jnp.int32, shape, 1)
    row = lax.broadcasted_iota(jnp.int32, shape, 0)
    blocks = []
    for i in range(count):
        part = corner[i * SUB : (i + 1) * SUB]
        unit = jnp.where(lane - width == row + i * SUB, 1.0, 0.0).astype(jnp.float32)
        blocks.append(jnp.where(lane < width, part, unit))
    for b in range(count):
        below = range(b + 1, count)
        spread = [
            {i: jnp.broadcast_to(blocks[i][:, b * SUB + j : b * SUB + j + 1], shape) for i in range(b, count)}
            for j in range(SUB)
        ]
        for j in range(SUB):
            pivot = jnp.broadcast_to(spread[j][b][j : j + 1, :], shape)
            scale = lax.rsqrt(pivot)
            scale = scale * (1.5 - 0.5 * (pivot * scale) * scale)
            top = jnp.broadcast_to(blocks[b][j : j + 1, :], shape) * scale
            factor = {i: spread[j][i] * scale for i in below}
            factor[b] = jnp.where(row > j, spread[j][b] * scale, 0.0)
            for k in range(j + 1, SUB):
                entry = jnp.broadcast_to(spread[k][b][j : j + 1, :], shape) * scale
                for i in range(b, count):
                    spread[k][i] = spread[k][i] - factor[i] * entry
            blocks[b] = jnp.where(row == j, top, blocks[b] - factor[b] * top)
            for i in below:
                blocks[i] = blocks[i] - factor[i] * top
    return jnp.concatenate([block[:, width:] for block in blocks], 0)


def pack_kernel(panel_ref, targets_ref, sent_ref):
    width = panel_ref.shape[0]
    for p in range(sent_ref.shape[0]):
        sent_ref[p, :width, :] = panel_ref[...]
        sent_ref[p, width:, :] = targets_ref[p]


def pack(panel, targets):
    count, mine, wide = targets.shape
    vmem = pl.BlockSpec(memory_space=pltpu.VMEM)
    return pl.pallas_call(
        pack_kernel,
        out_shape=jax.ShapeDtypeStruct((count, panel.shape[0] + mine, wide), jnp.float32),
        in_specs=[vmem, vmem],
        out_specs=vmem,
        name="pack_pieces",
    )(panel, targets)


def step_kernel(place_ref, pieces, kept_ref, arrived_ref, slab_panel_ref, panel_ref, slab_ref,
                slab_out, targets_out, factor_out, held, stacks, solved_targets, own_factor, arrive, leave, end):
    count, _, wide = pieces.shape
    width = panel_ref.shape[0]
    each = count // GROUPS
    loads, stores = [], []
    for g in range(GROUPS):
        rows = pl.ds(g * each * wide, each * wide)
        loads.append(pltpu.make_async_copy(slab_ref.at[rows], held.at[rows], arrive.at[g]))
        stores.append(pltpu.make_async_copy(held.at[rows], slab_out.at[rows], leave.at[g]))
    stores.append(pltpu.make_async_copy(own_factor, factor_out, end.at[0]))
    stores.append(pltpu.make_async_copy(solved_targets, targets_out, end.at[1]))
    for load in loads:
        load.start()
    is_first = place_ref[0] == 1
    lead_rows = jnp.where(place_ref[1] == 1, arrived_ref[...], kept_ref[...])
    inverse = inverse_factor(lead_rows[:width], width)
    slab_factor = exact(inverse, slab_panel_ref[...])
    high, low = halves(slab_factor)
    slab_stack = jnp.concatenate([high, low, high], 0)
    high, middle, low = thirds(inverse)
    large = jnp.concatenate([high, high, middle, middle], 1)
    small = jnp.concatenate([high, low], 1)
    for p in range(count):
        one, two, three = thirds(pieces[p, :width, :])
        solved = dot(large, jnp.concatenate([one, two, one, two], 0))
        solved = solved + dot(small, jnp.concatenate([three, one], 0))
        high, low = halves(solved)
        stacks[:, p * wide : (p + 1) * wide] = jnp.concatenate([high, high, low], 0)
    for g in range(GROUPS):
        loads[g].wait()
        for p in range(g * each, (g + 1) * each):
            product = dot(stacks[:, p * wide : (p + 1) * wide], slab_stack, ((0,), (0,)))
            held[p * wide : (p + 1) * wide, :] = held[p * wide : (p + 1) * wide, :] - product
        if g == 0:

            @pl.when(is_first)
            def _():
                held[:width, :] = slab_factor

        stores[g].start()
    own_factor[...] = exact(inverse, panel_ref[...])
    stores[GROUPS].start()
    lead = exact(lead_rows[width:, :width], inverse, ((1,), (1,)))
    high, low = halves(lead)
    lead_stack = jnp.concatenate([high, low, high], 1)
    for p in range(count):
        product = dot(lead_stack, stacks[:, p * wide : (p + 1) * wide])
        solved_targets[:, p * wide : (p + 1) * wide] = pieces[p, width:, :] - product

    @pl.when(is_first)
    def _():
        solved_targets[:, :width] = lead

    stores[GROUPS + 1].start()
    for store in stores:
        store.wait()


def step(place, got, kept, arrived, slab_panel, panel, slab):
    count, depth, wide = got.shape
    width = panel.shape[0]
    vmem = pl.BlockSpec(memory_space=pltpu.VMEM)
    hbm = pl.BlockSpec(memory_space=pl.ANY)
    outputs = (
        jax.ShapeDtypeStruct(slab.shape, jnp.float32),
        jax.ShapeDtypeStruct((depth - width, count * wide), jnp.float32),
        jax.ShapeDtypeStruct(panel.shape, jnp.float32),
    )
    return pl.pallas_call(
        step_kernel,
        out_shape=outputs,
        in_specs=[pl.BlockSpec(memory_space=pltpu.SMEM), vmem, vmem, vmem, vmem, vmem, hbm],
        out_specs=(hbm, hbm, hbm),
        scratch_shapes=[
            pltpu.VMEM(slab.shape, jnp.float32),
            pltpu.VMEM((3 * width, count * wide), jnp.bfloat16),
            pltpu.VMEM(outputs[1].shape, jnp.float32),
            pltpu.VMEM(panel.shape, jnp.float32),
            pltpu.SemaphoreType.DMA((GROUPS,)),
            pltpu.SemaphoreType.DMA((GROUPS,)),
            pltpu.SemaphoreType.DMA((2,)),
        ],
        compiler_params=pltpu.CompilerParams(vmem_limit_bytes=52 << 20),
        cost_estimate=pl.CostEstimate(
            flops=6 * slab.size * width, bytes_accessed=8 * slab.size, transcendentals=width
        ),
        name="factor_and_update",
    )(place, got, kept, arrived, slab_panel, panel, slab)


def body(kernel_panel, kernel_slab, targets):
    width, wide = kernel_panel.shape
    rows, cols = lax.axis_size("row"), lax.axis_size("col")
    row_index = lax.axis_index("row")
    mine = targets.shape[0] // cols

    def down(value):
        reach = 1
        while True:
            arrived = lax.ppermute(value, "row", [(i, i + reach) for i in range(reach)])
            new = (row_index >= reach) & (row_index < 2 * reach)
            reach = 2 * reach
            if reach == rows:
                return value, arrived, new
            value = jnp.where(new, arrived, value)

    sent = pack(kernel_panel, targets.reshape(cols, mine, wide))
    got = lax.all_to_all(sent, "col", split_axis=0, concat_axis=0)
    kept, arrived, new = down(kernel_slab[:width])
    slab_panel = jnp.where(new, arrived, kept)
    lead, slab_panel = lax.optimization_barrier((got[0, :, :LANES], slab_panel))
    kept, arrived, new = down(lead)
    place = jnp.stack([row_index == 0, new]).astype(jnp.int32)
    return tuple(step(place, got, kept, arrived, slab_panel, kernel_panel, kernel_slab))


def solution(mesh):
    in_specs = (P(None, ("row", "col")), P("row", "col"), P(None, ("row", "col")))
    out_specs = (P("row", "col"), P("col", "row"), P(None, ("row", "col")))
    return jax.shard_map(body, mesh=mesh, in_specs=in_specs, out_specs=out_specs, check_vma=False)
```

```python
import jax
import jax.numpy as jnp
from jax import lax
from jax.experimental import pallas as pl
from jax.experimental.pallas import tpu as pltpu
from jax.sharding import PartitionSpec as P

HIGHEST = lax.Precision.HIGHEST
LANES = 128
SUB = 8
GROUPS = 4


def dot(left, right, dims=((1,), (0,))):
    return lax.dot_general(left, right, (dims, ((), ())), preferred_element_type=jnp.float32)


def exact(left, right, dims=((1,), (0,))):
    return lax.dot_general(left, right, (dims, ((), ())), precision=HIGHEST, preferred_element_type=jnp.float32)


def halves(value):
    high = value.astype(jnp.bfloat16)
    return high, (value - high.astype(jnp.float32)).astype(jnp.bfloat16)


def thirds(value):
    high = value.astype(jnp.bfloat16)
    rest = value - high.astype(jnp.float32)
    return (high, *halves(rest))


def inverse_factor(corner, width):
    count = width // SUB
    shape = (SUB, LANES)
    lane = lax.broadcasted_iota(jnp.int32, shape, 1)
    row = lax.broadcasted_iota(jnp.int32, shape, 0)
    blocks = []
    for i in range(count):
        part = corner[i * SUB : (i + 1) * SUB]
        unit = jnp.where(lane - width == row + i * SUB, 1.0, 0.0).astype(jnp.float32)
        blocks.append(jnp.where(lane < width, part, unit))
    for b in range(count):
        below = range(b + 1, count)
        spread = [
            {i: jnp.broadcast_to(blocks[i][:, b * SUB + j : b * SUB + j + 1], shape) for i in range(b, count)}
            for j in range(SUB)
        ]
        for j in range(SUB):
            pivot = jnp.broadcast_to(spread[j][b][j : j + 1, :], shape)
            scale = lax.rsqrt(pivot)
            scale = scale * (1.5 - 0.5 * (pivot * scale) * scale)
            top = jnp.broadcast_to(blocks[b][j : j + 1, :], shape) * scale
            factor = {i: spread[j][i] * scale for i in below}
            factor[b] = jnp.where(row > j, spread[j][b] * scale, 0.0)
            for k in range(j + 1, SUB):
                entry = jnp.broadcast_to(spread[k][b][j : j + 1, :], shape) * scale
                for i in range(b, count):
                    spread[k][i] = spread[k][i] - factor[i] * entry
            blocks[b] = jnp.where(row == j, top, blocks[b] - factor[b] * top)
            for i in below:
                blocks[i] = blocks[i] - factor[i] * top
    return jnp.concatenate([block[:, width:] for block in blocks], 0)


def pack_kernel(panel_ref, targets_ref, *sent_refs):
    width = panel_ref.shape[0]
    for part, ref in enumerate(sent_refs):
        lanes = slice(part * LANES, (part + 1) * LANES)
        for p in range(ref.shape[0]):
            ref[p, :width, :] = panel_ref[:, lanes]
            ref[p, width:, :] = targets_ref[p, :, lanes]


def pack(panel, targets):
    count, mine, wide = targets.shape
    parts = wide // LANES
    vmem = pl.BlockSpec(memory_space=pltpu.VMEM)
    return pl.pallas_call(
        pack_kernel,
        out_shape=[jax.ShapeDtypeStruct((count, panel.shape[0] + mine, LANES), jnp.float32)] * parts,
        in_specs=[vmem, vmem],
        out_specs=[vmem] * parts,
        name="pack_pieces",
    )(panel, targets)


def step_kernel(place_ref, one_ref, two_ref, lead0_ref, lead1_ref, lead2_ref, lead3_ref, slab_ref,
                slab_out, targets_out, factor_out, held, stacks, solved_targets, own_factor, arrive, leave, end):
    count, depth, _ = one_ref.shape
    width, wide = own_factor.shape
    each = count // GROUPS
    loads, stores = [], []
    for g in range(GROUPS):
        rows = pl.ds(g * each * wide, each * wide)
        loads.append(pltpu.make_async_copy(slab_ref.at[rows], held.at[rows], arrive.at[g]))
        stores.append(pltpu.make_async_copy(held.at[rows], slab_out.at[rows], leave.at[g]))
    stores.append(pltpu.make_async_copy(own_factor, factor_out, end.at[0]))
    stores.append(pltpu.make_async_copy(solved_targets, targets_out, end.at[1]))
    for load in loads:
        load.start()
    is_first = place_ref[0] == 1
    lead_rows = lead0_ref[...]
    for number, ref in enumerate((lead1_ref, lead2_ref, lead3_ref)):
        lead_rows = jnp.where(place_ref[1] == number + 1, ref[...], lead_rows)
    inverse = inverse_factor(lead_rows[:width], width)
    slab_panel = jnp.concatenate([lead_rows[i : i + width] for i in range(depth, lead_rows.shape[0], width)], 1)
    slab_factor = exact(inverse, slab_panel)
    high, low = halves(slab_factor)
    slab_stack = jnp.concatenate([high, low, high], 0)
    high, middle, low = thirds(inverse)
    large = jnp.concatenate([high, high, middle, middle], 1)
    small = jnp.concatenate([high, low], 1)
    for p in range(count):
        one, two, three = thirds(jnp.concatenate([one_ref[p, :width, :], two_ref[p, :width, :]], 1))
        solved = dot(large, jnp.concatenate([one, two, one, two], 0))
        solved = solved + dot(small, jnp.concatenate([three, one], 0))
        high, low = halves(solved)
        stacks[:, p * wide : (p + 1) * wide] = jnp.concatenate([high, high, low], 0)
    for g in range(GROUPS):
        loads[g].wait()
        for p in range(g * each, (g + 1) * each):
            product = dot(stacks[:, p * wide : (p + 1) * wide], slab_stack, ((0,), (0,)))
            held[p * wide : (p + 1) * wide, :] = held[p * wide : (p + 1) * wide, :] - product
        if g == 0:

            @pl.when(is_first)
            def _():
                held[:width, :] = slab_factor

        stores[g].start()
    own_factor[...] = exact(inverse, jnp.concatenate([one_ref[place_ref[2], :width, :], two_ref[place_ref[2], :width, :]], 1))
    stores[GROUPS].start()
    lead = exact(lead_rows[width:depth, :width], inverse, ((1,), (1,)))
    high, low = halves(lead)
    lead_stack = jnp.concatenate([high, low, high], 1)
    for p in range(count):
        product = dot(lead_stack, stacks[:, p * wide : (p + 1) * wide])
        solved_targets[:, p * wide : (p + 1) * wide] = jnp.concatenate([one_ref[p, width:, :], two_ref[p, width:, :]], 1) - product

    @pl.when(is_first)
    def _():
        solved_targets[:, :width] = lead

    stores[GROUPS + 1].start()
    for store in stores:
        store.wait()


def step(place, one, two, leads, width, slab):
    count, depth, _ = one.shape
    wide = slab.shape[1]
    vmem = pl.BlockSpec(memory_space=pltpu.VMEM)
    hbm = pl.BlockSpec(memory_space=pl.ANY)
    outputs = (
        jax.ShapeDtypeStruct(slab.shape, jnp.float32),
        jax.ShapeDtypeStruct((depth - width, count * wide), jnp.float32),
        jax.ShapeDtypeStruct((width, wide), jnp.float32),
    )
    return pl.pallas_call(
        step_kernel,
        out_shape=outputs,
        in_specs=[pl.BlockSpec(memory_space=pltpu.SMEM), vmem, vmem, *[vmem] * len(leads), hbm],
        out_specs=(hbm, hbm, hbm),
        scratch_shapes=[
            pltpu.VMEM(slab.shape, jnp.float32),
            pltpu.VMEM((3 * width, count * wide), jnp.bfloat16),
            pltpu.VMEM(outputs[1].shape, jnp.float32),
            pltpu.VMEM(outputs[2].shape, jnp.float32),
            pltpu.SemaphoreType.DMA((GROUPS,)),
            pltpu.SemaphoreType.DMA((GROUPS,)),
            pltpu.SemaphoreType.DMA((2,)),
        ],
        compiler_params=pltpu.CompilerParams(vmem_limit_bytes=52 << 20),
        cost_estimate=pl.CostEstimate(
            flops=6 * slab.size * width, bytes_accessed=8 * slab.size, transcendentals=width
        ),
        name="factor_and_update",
    )(place, one, two, *leads, slab)


def body(kernel_panel, kernel_slab, targets):
    width, wide = kernel_panel.shape
    cols = lax.axis_size("col")
    row_index = lax.axis_index("row")
    mine = targets.shape[0] // cols

    first, second = pack(kernel_panel, targets.reshape(cols, mine, wide))
    first, slab = lax.optimization_barrier((first, kernel_slab))
    one = lax.all_to_all(first, "col", split_axis=0, concat_axis=0)
    two = lax.all_to_all(second, "col", split_axis=0, concat_axis=0)
    head = jnp.concatenate([slab[:width, at : at + LANES] for at in range(0, wide, LANES)], 0)
    one, head = lax.optimization_barrier((one, head))
    lead = jnp.concatenate([one[0], head], 0)
    arrived = lax.ppermute(lead, "row", [(0, 1)])
    leads = [jnp.where(row_index == 1, arrived, lead)]
    which = jnp.zeros_like(row_index)
    for i in (4, 2, 6):
        which = jnp.where(row_index // 2 * 2 == i, len(leads), which)
        leads.append(lax.ppermute(leads[0], "row", [(0, i), (1, i + 1)]))
    place = jnp.stack([(row_index == 0).astype(jnp.int32), which, lax.axis_index("col")])
    return tuple(step(place, one, two, leads, width, kernel_slab))


def solution(mesh):
    in_specs = (P(None, ("row", "col")), P("row", "col"), P(None, ("row", "col")))
    out_specs = (P("row", "col"), P("col", "row"), P(None, ("row", "col")))
    return jax.shard_map(body, mesh=mesh, in_specs=in_specs, out_specs=out_specs, check_vma=False)
```

```python
import jax
import jax.numpy as jnp
from jax import lax
from jax.experimental import pallas as pl
from jax.experimental.pallas import tpu as pltpu
from jax.sharding import PartitionSpec as P

HIGHEST = lax.Precision.HIGHEST
LANES = 128
SUB = 8
GROUPS = 4


def dot(left, right, dims=((1,), (0,))):
    return lax.dot_general(left, right, (dims, ((), ())), preferred_element_type=jnp.float32)


def exact(left, right, dims=((1,), (0,))):
    return lax.dot_general(left, right, (dims, ((), ())), precision=HIGHEST, preferred_element_type=jnp.float32)


def halves(value):
    high = value.astype(jnp.bfloat16)
    return high, (value - high.astype(jnp.float32)).astype(jnp.bfloat16)


def thirds(value):
    high = value.astype(jnp.bfloat16)
    rest = value - high.astype(jnp.float32)
    return (high, *halves(rest))


def inverse_factor(corner, width):
    count = width // SUB
    shape = (SUB, LANES)
    lane = lax.broadcasted_iota(jnp.int32, shape, 1)
    row = lax.broadcasted_iota(jnp.int32, shape, 0)
    blocks = []
    for i in range(count):
        part = corner[i * SUB : (i + 1) * SUB]
        unit = jnp.where(lane - width == row + i * SUB, 1.0, 0.0).astype(jnp.float32)
        blocks.append(jnp.where(lane < width, part, unit))
    for b in range(count):
        below = range(b + 1, count)
        spread = [
            {i: jnp.broadcast_to(blocks[i][:, b * SUB + j : b * SUB + j + 1], shape) for i in range(b, count)}
            for j in range(SUB)
        ]
        for j in range(SUB):
            pivot = jnp.broadcast_to(spread[j][b][j : j + 1, :], shape)
            scale = lax.rsqrt(pivot)
            top = jnp.broadcast_to(blocks[b][j : j + 1, :], shape) * scale
            factor = {i: spread[j][i] * scale for i in below}
            factor[b] = jnp.where(row > j, spread[j][b] * scale, 0.0)
            for k in range(j + 1, SUB):
                entry = jnp.broadcast_to(spread[k][b][j : j + 1, :], shape) * scale
                for i in range(b, count):
                    spread[k][i] = spread[k][i] - factor[i] * entry
            blocks[b] = jnp.where(row == j, top, blocks[b] - factor[b] * top)
            for i in below:
                blocks[i] = blocks[i] - factor[i] * top
    return jnp.concatenate([block[:, width:] for block in blocks], 0)


def pack_kernel(panel_ref, targets_ref, sent_ref):
    width = panel_ref.shape[0]
    for p in range(sent_ref.shape[0]):
        sent_ref[p, :width, :] = panel_ref[...]
        sent_ref[p, width:, :] = targets_ref[p]


def pack(panel, targets, part):
    count, mine, _ = targets.shape
    width = panel.shape[0]
    sent = (count, width + mine, LANES)
    return pl.pallas_call(
        pack_kernel,
        grid=(1,),
        out_shape=jax.ShapeDtypeStruct(sent, jnp.float32),
        in_specs=[
            pl.BlockSpec((width, LANES), lambda i: (0, part)),
            pl.BlockSpec((count, mine, LANES), lambda i: (0, 0, part)),
        ],
        out_specs=pl.BlockSpec(sent, lambda i: (0, 0, 0)),
        name="pack_pieces",
    )(panel, targets)


def step_kernel(place_ref, one_ref, two_ref, lead0_ref, lead1_ref, lead2_ref, lead3_ref, slab_ref,
                slab_out, targets_out, factor_out, held, stacks, solved_targets, own_factor, arrive, leave, end):
    count, depth, _ = one_ref.shape
    width, wide = own_factor.shape
    each = count // GROUPS
    loads, stores = [], []
    for g in range(GROUPS):
        rows = pl.ds(g * each * wide, each * wide)
        loads.append(pltpu.make_async_copy(slab_ref.at[rows], held.at[rows], arrive.at[g]))
        stores.append(pltpu.make_async_copy(held.at[rows], slab_out.at[rows], leave.at[g]))
    stores.append(pltpu.make_async_copy(own_factor, factor_out, end.at[0]))
    stores.append(pltpu.make_async_copy(solved_targets, targets_out, end.at[1]))
    for load in loads:
        load.start()
    is_first = place_ref[0] == 1
    lead_rows = lead0_ref[...]
    for number, ref in enumerate((lead1_ref, lead2_ref, lead3_ref)):
        lead_rows = jnp.where(place_ref[1] == number + 1, ref[...], lead_rows)
    inverse = inverse_factor(lead_rows[:width], width)
    slab_panel = jnp.concatenate([lead_rows[i : i + width] for i in range(depth, lead_rows.shape[0], width)], 1)
    slab_factor = exact(inverse, slab_panel)
    high, low = halves(slab_factor)
    slab_stack = jnp.concatenate([high, low, high], 0)
    high, middle, low = thirds(inverse)
    large = jnp.concatenate([high, high, middle, middle], 1)
    small = jnp.concatenate([high, low], 1)
    for p in range(count):
        one, two, three = thirds(jnp.concatenate([one_ref[p, :width, :], two_ref[p, :width, :]], 1))
        solved = dot(large, jnp.concatenate([one, two, one, two], 0))
        solved = solved + dot(small, jnp.concatenate([three, one], 0))
        high, low = halves(solved)
        stacks[:, p * wide : (p + 1) * wide] = jnp.concatenate([high, high, low], 0)
    for g in range(GROUPS):
        loads[g].wait()
        for p in range(g * each, (g + 1) * each):
            product = dot(stacks[:, p * wide : (p + 1) * wide], slab_stack, ((0,), (0,)))
            held[p * wide : (p + 1) * wide, :] = held[p * wide : (p + 1) * wide, :] - product
        if g == 0:

            @pl.when(is_first)
            def _():
                held[:width, :] = slab_factor

        stores[g].start()
    own_factor[...] = exact(inverse, jnp.concatenate([one_ref[place_ref[2], :width, :], two_ref[place_ref[2], :width, :]], 1))
    stores[GROUPS].start()
    lead = exact(lead_rows[width:depth, :width], inverse, ((1,), (1,)))
    high, low = halves(lead)
    lead_stack = jnp.concatenate([high, low, high], 1)
    for p in range(count):
        product = dot(lead_stack, stacks[:, p * wide : (p + 1) * wide])
        solved_targets[:, p * wide : (p + 1) * wide] = jnp.concatenate([one_ref[p, width:, :], two_ref[p, width:, :]], 1) - product

    @pl.when(is_first)
    def _():
        solved_targets[:, :width] = lead

    stores[GROUPS + 1].start()
    for store in stores:
        store.wait()


def step(place, one, two, leads, width, slab):
    count, depth, _ = one.shape
    wide = slab.shape[1]
    vmem = pl.BlockSpec(memory_space=pltpu.VMEM)
    hbm = pl.BlockSpec(memory_space=pl.ANY)
    outputs = (
        jax.ShapeDtypeStruct(slab.shape, jnp.float32),
        jax.ShapeDtypeStruct((depth - width, count * wide), jnp.float32),
        jax.ShapeDtypeStruct((width, wide), jnp.float32),
    )
    return pl.pallas_call(
        step_kernel,
        out_shape=outputs,
        in_specs=[pl.BlockSpec(memory_space=pltpu.SMEM), vmem, vmem, *[vmem] * len(leads), hbm],
        out_specs=(hbm, hbm, hbm),
        scratch_shapes=[
            pltpu.VMEM(slab.shape, jnp.float32),
            pltpu.VMEM((3 * width, count * wide), jnp.bfloat16),
            pltpu.VMEM(outputs[1].shape, jnp.float32),
            pltpu.VMEM(outputs[2].shape, jnp.float32),
            pltpu.SemaphoreType.DMA((GROUPS,)),
            pltpu.SemaphoreType.DMA((GROUPS,)),
            pltpu.SemaphoreType.DMA((2,)),
        ],
        compiler_params=pltpu.CompilerParams(vmem_limit_bytes=52 << 20),
        cost_estimate=pl.CostEstimate(
            flops=6 * slab.size * width, bytes_accessed=8 * slab.size, transcendentals=width
        ),
        name="factor_and_update",
    )(place, one, two, *leads, slab)


def body(kernel_panel, kernel_slab, targets):
    width, wide = kernel_panel.shape
    cols = lax.axis_size("col")
    row_index = lax.axis_index("row")
    mine = targets.shape[0] // cols

    target_rows = targets.reshape(cols, mine, wide)
    first = pack(kernel_panel, target_rows, 0)
    first, panel, target_rows, slab = lax.optimization_barrier((first, kernel_panel, target_rows, kernel_slab))
    second = pack(panel, target_rows, 1)
    one = lax.all_to_all(first, "col", split_axis=0, concat_axis=0)
    head = jnp.concatenate([slab[:width, at : at + LANES] for at in range(0, wide, LANES)], 0)
    one, head, second = lax.optimization_barrier((one, head, second))
    two = lax.all_to_all(second, "col", split_axis=0, concat_axis=0)
    lead = jnp.concatenate([one[0], head], 0)
    arrived = lax.ppermute(lead, "row", [(0, 1)])
    leads = [jnp.where(row_index == 1, arrived, lead)]
    which = jnp.zeros_like(row_index)
    for i in (4, 2, 6):
        which = jnp.where(row_index // 2 * 2 == i, len(leads), which)
        leads.append(lax.ppermute(leads[0], "row", [(0, i), (1, i + 1)]))
    place = jnp.stack([(row_index == 0).astype(jnp.int32), which, lax.axis_index("col")])
    return tuple(step(place, one, two, leads, width, kernel_slab))


def solution(mesh):
    in_specs = (P(None, ("row", "col")), P("row", "col"), P(None, ("row", "col")))
    out_specs = (P("row", "col"), P("col", "row"), P(None, ("row", "col")))
    return jax.shard_map(body, mesh=mesh, in_specs=in_specs, out_specs=out_specs, check_vma=False)
```

```python
import jax
import jax.numpy as jnp
from jax import lax
from jax.experimental import pallas as pl
from jax.experimental.pallas import tpu as pltpu
from jax.sharding import PartitionSpec as P

HIGHEST = lax.Precision.HIGHEST
LANES = 128
SUB = 8
GROUPS = 4


def dot(left, right, dims=((1,), (0,))):
    return lax.dot_general(left, right, (dims, ((), ())), preferred_element_type=jnp.float32)


def exact(left, right, dims=((1,), (0,))):
    return lax.dot_general(left, right, (dims, ((), ())), precision=HIGHEST, preferred_element_type=jnp.float32)


def halves(value):
    high = value.astype(jnp.bfloat16)
    return high, (value - high.astype(jnp.float32)).astype(jnp.bfloat16)


def thirds(value):
    high = value.astype(jnp.bfloat16)
    rest = value - high.astype(jnp.float32)
    return (high, *halves(rest))


def inverse_factor(corner, width):
    count = width // SUB
    shape = (SUB, LANES)
    lane = lax.broadcasted_iota(jnp.int32, shape, 1)
    row = lax.broadcasted_iota(jnp.int32, shape, 0)
    blocks = []
    for i in range(count):
        part = corner[i * SUB : (i + 1) * SUB]
        unit = jnp.where(lane - width == row + i * SUB, 1.0, 0.0).astype(jnp.float32)
        blocks.append(jnp.where(lane < width, part, unit))
    for b in range(count):
        below = range(b + 1, count)
        spread = [
            {i: jnp.broadcast_to(blocks[i][:, b * SUB + j : b * SUB + j + 1], shape) for i in range(b, count)}
            for j in range(SUB)
        ]
        for j in range(SUB):
            pivot = jnp.broadcast_to(spread[j][b][j : j + 1, :], shape)
            scale = lax.rsqrt(pivot)
            top = jnp.broadcast_to(blocks[b][j : j + 1, :], shape) * scale
            factor = {i: spread[j][i] * scale for i in below}
            factor[b] = jnp.where(row > j, spread[j][b] * scale, 0.0)
            for k in range(j + 1, SUB):
                entry = jnp.broadcast_to(spread[k][b][j : j + 1, :], shape) * scale
                for i in range(b, count):
                    spread[k][i] = spread[k][i] - factor[i] * entry
            blocks[b] = jnp.where(row == j, top, blocks[b] - factor[b] * top)
            for i in below:
                blocks[i] = blocks[i] - factor[i] * top
    return jnp.concatenate([block[:, width:] for block in blocks], 0)


def pack_kernel(panel_ref, targets_ref, sent_ref):
    width = panel_ref.shape[0]
    for p in range(sent_ref.shape[0]):
        sent_ref[p, :width, :] = panel_ref[...]
        sent_ref[p, width:, :] = targets_ref[p]


def pack(panel, targets, part):
    count, mine, _ = targets.shape
    width = panel.shape[0]
    sent = (count, width + mine, LANES)
    return pl.pallas_call(
        pack_kernel,
        grid=(1,),
        out_shape=jax.ShapeDtypeStruct(sent, jnp.float32),
        in_specs=[
            pl.BlockSpec((width, LANES), lambda i: (0, part)),
            pl.BlockSpec((count, mine, LANES), lambda i: (0, 0, part)),
        ],
        out_specs=pl.BlockSpec(sent, lambda i: (0, 0, 0)),
        name="pack_pieces",
    )(panel, targets)


def step_kernel(place_ref, one_ref, two_ref, lead0_ref, lead1_ref, lead2_ref, lead3_ref, slab_ref,
                slab_out, targets_out, factor_out, held, parts, stacks, solved_targets, own_factor, arrive, leave, end):
    count, depth, _ = one_ref.shape
    width, wide = own_factor.shape
    each = count // GROUPS
    loads, stores = [], []
    for g in range(GROUPS):
        rows = pl.ds(g * each * wide, each * wide)
        loads.append(pltpu.make_async_copy(slab_ref.at[rows], held.at[rows], arrive.at[g]))
        stores.append(pltpu.make_async_copy(held.at[rows], slab_out.at[rows], leave.at[g]))
    stores.append(pltpu.make_async_copy(own_factor, factor_out, end.at[0]))
    stores.append(pltpu.make_async_copy(solved_targets, targets_out, end.at[1]))
    for load in loads:
        load.start()
    is_first = place_ref[0] == 1
    lead_rows = lead0_ref[...]
    for number, ref in enumerate((lead1_ref, lead2_ref, lead3_ref)):
        lead_rows = jnp.where(place_ref[1] == number + 1, ref[...], lead_rows)
    for p in range(count):
        one, two, three = thirds(jnp.concatenate([one_ref[p, :width, :], two_ref[p, :width, :]], 1))
        for i, part in enumerate((one, two, three, one)):
            parts[i * width : (i + 1) * width, p * wide : (p + 1) * wide] = part
    inverse = inverse_factor(lead_rows[:width], width)
    slab_panel = jnp.concatenate([lead_rows[i : i + width] for i in range(depth, lead_rows.shape[0], width)], 1)
    slab_factor = exact(inverse, slab_panel)
    high, low = halves(slab_factor)
    slab_stack = jnp.concatenate([high, low, high], 0)
    high, middle, low = thirds(inverse)
    large = jnp.concatenate([high, high, high, middle], 1)
    small = jnp.concatenate([low, middle], 1)
    for p in range(count):
        piece = parts[:, p * wide : (p + 1) * wide]
        solved = dot(large, piece) + dot(small, piece[: 2 * width])
        high, low = halves(solved)
        stacks[:, p * wide : (p + 1) * wide] = jnp.concatenate([high, high, low], 0)
    for g in range(GROUPS):
        loads[g].wait()
        for p in range(g * each, (g + 1) * each):
            product = dot(stacks[:, p * wide : (p + 1) * wide], slab_stack, ((0,), (0,)))
            held[p * wide : (p + 1) * wide, :] = held[p * wide : (p + 1) * wide, :] - product
        if g == 0:

            @pl.when(is_first)
            def _():
                held[:width, :] = slab_factor

        stores[g].start()
    own_factor[...] = exact(inverse, jnp.concatenate([one_ref[place_ref[2], :width, :], two_ref[place_ref[2], :width, :]], 1))
    stores[GROUPS].start()
    lead = exact(lead_rows[width:depth, :width], inverse, ((1,), (1,)))
    high, low = halves(lead)
    lead_stack = jnp.concatenate([high, low, high], 1)
    for p in range(count):
        product = dot(lead_stack, stacks[:, p * wide : (p + 1) * wide])
        solved_targets[:, p * wide : (p + 1) * wide] = jnp.concatenate([one_ref[p, width:, :], two_ref[p, width:, :]], 1) - product

    @pl.when(is_first)
    def _():
        solved_targets[:, :width] = lead

    stores[GROUPS + 1].start()
    for store in stores:
        store.wait()


def step(place, one, two, leads, width, slab):
    count, depth, _ = one.shape
    wide = slab.shape[1]
    vmem = pl.BlockSpec(memory_space=pltpu.VMEM)
    hbm = pl.BlockSpec(memory_space=pl.ANY)
    outputs = (
        jax.ShapeDtypeStruct(slab.shape, jnp.float32),
        jax.ShapeDtypeStruct((depth - width, count * wide), jnp.float32),
        jax.ShapeDtypeStruct((width, wide), jnp.float32),
    )
    return pl.pallas_call(
        step_kernel,
        out_shape=outputs,
        in_specs=[pl.BlockSpec(memory_space=pltpu.SMEM), vmem, vmem, *[vmem] * len(leads), hbm],
        out_specs=(hbm, hbm, hbm),
        scratch_shapes=[
            pltpu.VMEM(slab.shape, jnp.float32),
            pltpu.VMEM((4 * width, count * wide), jnp.bfloat16),
            pltpu.VMEM((3 * width, count * wide), jnp.bfloat16),
            pltpu.VMEM(outputs[1].shape, jnp.float32),
            pltpu.VMEM(outputs[2].shape, jnp.float32),
            pltpu.SemaphoreType.DMA((GROUPS,)),
            pltpu.SemaphoreType.DMA((GROUPS,)),
            pltpu.SemaphoreType.DMA((2,)),
        ],
        compiler_params=pltpu.CompilerParams(vmem_limit_bytes=52 << 20),
        cost_estimate=pl.CostEstimate(
            flops=6 * slab.size * width, bytes_accessed=8 * slab.size, transcendentals=width
        ),
        name="factor_and_update",
    )(place, one, two, *leads, slab)


def body(kernel_panel, kernel_slab, targets):
    width, wide = kernel_panel.shape
    cols = lax.axis_size("col")
    row_index = lax.axis_index("row")
    mine = targets.shape[0] // cols

    target_rows = targets.reshape(cols, mine, wide)
    first = pack(kernel_panel, target_rows, 0)
    first, panel, target_rows, slab = lax.optimization_barrier((first, kernel_panel, target_rows, kernel_slab))
    second = pack(panel, target_rows, 1)
    one = lax.all_to_all(first, "col", split_axis=0, concat_axis=0)
    head = jnp.concatenate([slab[:width, at : at + LANES] for at in range(0, wide, LANES)], 0)
    one, head, second = lax.optimization_barrier((one, head, second))
    two = lax.all_to_all(second, "col", split_axis=0, concat_axis=0)
    lead = jnp.concatenate([one[0], head], 0)
    arrived = lax.ppermute(lead, "row", [(0, 1)])
    leads = [jnp.where(row_index == 1, arrived, lead)]
    which = jnp.zeros_like(row_index)
    for i in (6, 4, 2):
        which = jnp.where(row_index // 2 * 2 == i, len(leads), which)
        leads.append(lax.ppermute(leads[0], "row", [(0, i), (1, i + 1)]))
    place = jnp.stack([(row_index == 0).astype(jnp.int32), which, lax.axis_index("col")])
    return tuple(step(place, one, two, leads, width, kernel_slab))


def solution(mesh):
    in_specs = (P(None, ("row", "col")), P("row", "col"), P(None, ("row", "col")))
    out_specs = (P("row", "col"), P("col", "row"), P(None, ("row", "col")))
    return jax.shard_map(body, mesh=mesh, in_specs=in_specs, out_specs=out_specs, check_vma=False)
```
